32 devices in a mesh: req: 8 (over z, x), cfg: 2 (over core), seq: 2 (over y).
Axes of the slice: x: 2, y: 2, z: 4, core: 2. Of those that a mesh axis runs over, the one named last changes fastest.
Arguments:
- queries: bfloat16 [8, 2, 512, 1024], P('req', 'cfg', 'seq'), may hold values from -48 to 48
- key_vectors: bfloat16 [8, 2, 512, 1024], P('req', 'cfg', 'seq'), may hold values from -48 to 48
- values: bfloat16 [8, 2, 512, 1024], P('req', 'cfg', 'seq'), may hold values from -6 to 6
- hidden: bfloat16 [8, 2, 512, 1536], P('req', 'cfg', 'seq'), may hold values from -15 to 15
- out_proj: bfloat16 [1024, 1536], P('req'), may hold values from -0.1875 to 0.1875
- head_weight: bfloat16 [1536, 64], replicated, may hold values from -0.15625 to 0.15625
- head_bias: float32 [64], replicated, may hold values from -3 to 3
- attn_gate: float32 [8, 1536], P('req'), may hold values from 0.5 to 4
- shift_scale: float32 [8, 2, 1536], P('req'), may hold values from -3 to 3
- grid_shape: int32 [8, 3], P('req'), may hold values from 1 to 32, as said below
- step_index: int32 [8], P('req'), may hold values from 0 to 19
- guide_scale: float32 [8], P('req'), may hold values from 3 to 6
- latent: float32 [8, 512, 64], P('req', 'seq', 'cfg'), may hold values from -6 to 6
Outputs:
- next_latent: float32 [8, 512, 64], P('req', 'seq', 'cfg')
- velocity: float32 [8, 512, 64], P('req', 'seq', 'cfg')
The draws below stay inside these ranges and needn't reach their ends.
Inputs may be any that keep to these rules, and one draw needn't show every extreme that they name: `grid_shape`: the frames are at most 2, the height at most 8 and the width at most 32, so that frames * height * width is at most 512; in every draw some request fills all 512 slots.
All inputs are finite; a program needn't handle non-finite values.
Results may differ from the reference program's by a relative error of at most 0.0052.
Values may be sent and summed in bfloat16 or wider, within the bound.
A program may use at most 64 MiB of HBM per device.

```python
import math
import jax
import jax.numpy as jnp
from jax import lax

D = 1536
HEADS = 8
HEAD_DIM = 128
CH = 64
STEPS = 20
TOK_DEV = 256
SEQ_LEN = 512
REQS = 8


def draw_queries(key, part):
    shape = (REQS, 2, SEQ_LEN, HEADS * HEAD_DIM)
    subkey = jax.random.fold_in(key, 11)
    base = jnp.clip(2.0 * jax.random.normal(subkey, shape, jnp.float32), -12.0, 12.0)
    return base.astype(jnp.bfloat16)


def draw_key_vectors(key, part):
    shape = (REQS, 2, SEQ_LEN, HEADS * HEAD_DIM)
    subkey = jax.random.fold_in(key, 23)
    base = jnp.clip(jax.random.normal(subkey, shape, jnp.float32), -6.0, 6.0)
    return base.astype(jnp.bfloat16)


def draw_hidden(key, part):
    subkeys = jax.random.split(jax.random.fold_in(key, 37), 3)
    low = math.log(0.5)
    high = math.log(5.0)
    row_scale = jnp.exp(jax.random.uniform(subkeys[0], (REQS, 2, SEQ_LEN, 1), jnp.float32, low, high))
    col_scale = jnp.exp(jax.random.uniform(subkeys[1], (1, 1, 1, D), jnp.float32, low, high))
    shape = (REQS, 2, SEQ_LEN, D)
    base = jnp.clip(jax.random.normal(subkeys[2], shape, jnp.float32), -4.0, 4.0)
    return (0.15 * row_scale * col_scale * base).astype(jnp.bfloat16)


def draw_grid_shape(key, part):
    subkeys = jax.random.split(jax.random.fold_in(key, 41), 4)
    most_frames = SEQ_LEN // TOK_DEV
    frames = jax.random.randint(subkeys[0], (REQS,), max(1, most_frames // 2), most_frames + 1)
    height = jax.random.randint(subkeys[1], (REQS,), 4, 9)
    across = jax.random.randint(subkeys[2], (REQS,), max(1, TOK_DEV // 16), TOK_DEV // 8 + 1)
    chosen = jax.random.randint(subkeys[3], (), 0, REQS)
    filled = jnp.arange(REQS, dtype=jnp.int32) == chosen
    frames = jnp.where(filled, most_frames, frames)
    height = jnp.where(filled, 8, height)
    across = jnp.where(filled, TOK_DEV // 8, across)
    return jnp.stack([frames, height, across], axis=1).astype(jnp.int32)


def touch_ends(drawn, own_key, smallest, top_value):
    place = [jax.random.randint(jax.random.fold_in(own_key, axis), (), 0, length) for axis, length in enumerate(drawn.shape)]
    widest = drawn.shape.index(max(drawn.shape))
    next_to = place[:widest] + [(place[widest] + 1) % drawn.shape[widest]] + place[widest + 1:]
    return drawn.at[tuple(place)].set(smallest).at[tuple(next_to)].set(top_value)


def block_scale(key, shape, cuts, least, largest):
    gain, own = 1.0, jax.random.fold_in(key, 6)
    for dim, shards_of in cuts:
        draws = jnp.exp(jax.random.uniform(jax.random.fold_in(own, dim), (shards_of,), jnp.float32, least / len(cuts), largest / len(cuts)))
        gain = gain * jnp.repeat(draws, shape[dim] // shards_of).reshape([-1 if axis == dim else 1 for axis in range(len(shape))])
    return gain


def normal_values(own_key, dims, scale, reach, shards=(), kind=jnp.bfloat16):
    drawn = scale * jax.random.normal(own_key, dims, jnp.float32)
    if shards:
        drawn = drawn * block_scale(own_key, dims, shards, -0.22, 0.18)
    return jnp.clip(drawn, -reach, reach).astype(kind)


def setup_inputs(seed: int = 0) -> dict:
    key_list = jax.random.split(jax.random.key(seed), 14)
    return {
        "queries": draw_queries(jax.random.fold_in(key_list[13], 71), 0),
        "key_vectors": draw_key_vectors(jax.random.fold_in(key_list[13], 71), 0),
        "values": normal_values(key_list[2], (REQS, 2, SEQ_LEN, HEADS * HEAD_DIM), 1.0, 6.0, ((0, 8), (1, 2), (2, 2))),
        "hidden": draw_hidden(jax.random.fold_in(key_list[13], 71), 0),
        "out_proj": normal_values(key_list[4], (HEADS * HEAD_DIM, D), (HEADS * HEAD_DIM) ** -0.5, 0.1875, ((0, 8),)),
        "head_weight": normal_values(key_list[5], (D, CH), D ** -0.5, 0.15625),
        "head_bias": normal_values(key_list[6], (CH,), 0.5, 3.0, (), jnp.float32),
        "attn_gate": jnp.clip(jnp.exp(math.log(4.0) - 2.0794415 * jax.random.uniform(key_list[7], (REQS, D), jnp.float32) ** block_scale(key_list[7], (REQS, D), ((0, 8),), -0.2, 0.2)), 0.5, 4.0),
        "shift_scale": normal_values(key_list[8], (REQS, 2, D), 0.5, 3.0, ((0, 8),), jnp.float32),
        "grid_shape": draw_grid_shape(jax.random.fold_in(key_list[13], 71), 0),
        "step_index": touch_ends(jax.random.randint(key_list[10], (REQS,), 0, STEPS), jax.random.fold_in(key_list[10], 1), 0, STEPS - 1).astype(jnp.int32),
        "guide_scale": jnp.clip(3.0 + 3.0 * jax.random.uniform(key_list[11], (REQS,), jnp.float32) ** block_scale(key_list[11], (REQS,), ((0, 8),), -0.2, 0.2), 3.0, 6.0),
        "latent": normal_values(key_list[12], (REQS, SEQ_LEN, CH), 1.0, 6.0, ((0, 8), (1, 2), (2, 2)), jnp.float32),
    }


masked_score = -1e+30
norm_eps = 1e-06
shift_factor = 5.0

def rotary(vectors, grid_dims, first_token):
    row_count, col_count = vectors.shape
    sixth_dim = HEAD_DIM // 6
    time_pairs = (HEAD_DIM - 4 * sixth_dim) // 2
    column = jnp.arange(col_count, dtype=jnp.int32) % HEAD_DIM
    pair_index = column // 2
    space_pair = (pair_index - time_pairs).astype(jnp.float32)
    is_time = pair_index < time_pairs
    is_height = jnp.logical_and(pair_index >= time_pairs, pair_index < time_pairs + sixth_dim)
    exponent = jnp.where(is_time, pair_index.astype(jnp.float32) / time_pairs, jnp.where(is_height, space_pair / sixth_dim, (space_pair - sixth_dim) / sixth_dim))
    frequency = jnp.power(jnp.float32(10000.0), -exponent)
    token_ids = first_token + jnp.arange(row_count, dtype=jnp.int32)
    plane_size = grid_dims[1] * grid_dims[2]
    frame_ids = token_ids // plane_size
    height = token_ids // grid_dims[2] % grid_dims[1]
    across = token_ids % grid_dims[2]
    position = jnp.where(is_time[None, :], frame_ids[:, None], jnp.where(is_height[None, :], height[:, None], across[:, None])).astype(jnp.float32)
    angles = position * frequency[None, :]
    is_even = column % 2 == 0
    source = vectors.astype(jnp.float32)
    partner = jnp.where(is_even[None, :], jnp.roll(source, -1, axis=1), jnp.roll(source, 1, axis=1))
    sign_flip = jnp.where(is_even, -1.0, 1.0).astype(jnp.float32)
    turned = source * jnp.cos(angles) + partner * (jnp.sin(angles) * sign_flip[None, :])
    return turned.astype(jnp.bfloat16)

def noise_level(step_value):
    progress = 1.0 - step_value.astype(jnp.float32) / STEPS
    return shift_factor * progress / (1.0 + (shift_factor - 1.0) * progress)

def output_head(hidden_rows, proj, gate_row, modulation, head_weight, head_bias):
    mixed_rows = hidden_rows.astype(jnp.float32) + gate_row[None, :] * proj
    average = lax.optimization_barrier(jnp.mean(mixed_rows, axis=-1, keepdims=True))
    centered = mixed_rows - average
    spread = lax.optimization_barrier(jnp.mean(centered * centered, axis=-1, keepdims=True))
    normed = centered * lax.rsqrt(spread + norm_eps)
    modded = (normed * (1.0 + modulation[1][None, :]) + modulation[0][None, :]).astype(jnp.bfloat16)
    return jnp.dot(modded, head_weight, preferred_element_type=jnp.float32) + head_bias[None, :]

def attend(rot_q, rot_k, value_rows, length):
    total_rows = rot_q.shape[0]
    block_rows = min(512, total_rows)
    score_scale = 1.0 / math.sqrt(HEAD_DIM)
    query_heads = rot_q.astype(jnp.float32).reshape(total_rows, HEADS, HEAD_DIM)
    key_heads = rot_k.astype(jnp.float32).reshape(total_rows, HEADS, HEAD_DIM)
    value_heads = value_rows.astype(jnp.float32).reshape(total_rows, HEADS, HEAD_DIM)
    live_keys = jnp.arange(total_rows, dtype=jnp.int32) < length

    def one_block(start):
        query_block = lax.dynamic_slice_in_dim(query_heads, start, block_rows, 0)
        scores = jnp.einsum('qhd,khd->hqk', query_block, key_heads) * score_scale
        scores = jnp.where(live_keys[None, None, :], scores, masked_score)
        row_max = lax.optimization_barrier(jnp.max(scores, axis=-1, keepdims=True))
        exponent = jnp.exp(scores - row_max)
        row_sum = lax.optimization_barrier(jnp.sum(exponent, axis=-1, keepdims=True))
        weights = lax.optimization_barrier((exponent / row_sum).astype(jnp.bfloat16))
        output = jnp.einsum('hqk,khd->qhd', weights.astype(jnp.float32), value_heads)
        return output.astype(jnp.bfloat16)
    starts = jnp.arange(total_rows // block_rows, dtype=jnp.int32) * block_rows
    blocks = lax.map(one_block, starts)
    return blocks.reshape(total_rows, HEADS * HEAD_DIM)

def reference(queries, key_vectors, values, hidden, out_proj, head_weight, head_bias, attn_gate, shift_scale, grid_shape, step_index, guide_scale, latent):

    def one_request(request_items):
        query_req, key_req, value_req, hidden_req, gate_row, modulation, grid_dims, step_value, guide_value, latent_req = request_items
        length = grid_dims[0] * grid_dims[1] * grid_dims[2]
        predictions = []
        for cfg_half in range(2):
            rot_q = lax.optimization_barrier(rotary(query_req[cfg_half], grid_dims, 0))
            rot_k = lax.optimization_barrier(rotary(key_req[cfg_half], grid_dims, 0))
            attended = attend(rot_q, rot_k, value_req[cfg_half], length)
            proj = jnp.dot(attended, out_proj, preferred_element_type=jnp.float32)
            predictions.append(output_head(hidden_req[cfg_half], proj, gate_row, modulation, head_weight, head_bias))
        guided = predictions[1] + guide_value * (predictions[0] - predictions[1])
        live_rows = jnp.arange(guided.shape[0], dtype=jnp.int32) < length
        velocity = jnp.where(live_rows[:, None], guided, jnp.float32(0.0))
        delta_level = noise_level(step_value + 1) - noise_level(step_value)
        return (latent_req + delta_level * velocity, velocity)
    return lax.map(one_request, (queries, key_vectors, values, hidden, attn_gate, shift_scale, grid_shape, step_index, guide_scale, latent))
```

```python
import functools
import math

import jax
import jax.numpy as jnp
from jax import lax
from jax.experimental import pallas as pl
from jax.experimental.pallas import tpu as pltpu
from jax.sharding import PartitionSpec as P

HEAD_DIM = 128
STEPS = 20
PAIR = 2 * HEAD_DIM

masked_score = -1e30
norm_eps = 1e-06
shift_factor = 5.0
MESH = pl.DeviceIdType.MESH


def noise_level(step_value):
    progress = 1.0 - step_value / STEPS
    return shift_factor * progress / (1.0 + (shift_factor - 1.0) * progress)


def fill_tables(cos_ref, sin_ref, start, rows, first_token, dims):
    height, width = dims
    sixth = HEAD_DIM // 6
    time_pairs = (HEAD_DIM - 4 * sixth) // 2
    lane = lax.broadcasted_iota(jnp.int32, (8, HEAD_DIM), 1)
    pair = lane // 2
    is_time = pair < time_pairs
    is_row = pair < time_pairs + sixth
    pair_f = pair.astype(jnp.float32)
    space = pair_f - time_pairs
    exponent = jnp.where(
        is_time, pair_f / time_pairs, jnp.where(is_row, space / sixth, (space - sixth) / sixth)
    )
    freq = jnp.exp(exponent * -math.log(10000.0))[0:1]
    sign = jnp.where(lane % 2 == 0, -1.0, 1.0).astype(jnp.float32)[0:1]
    lanes = lax.broadcasted_iota(jnp.int32, (rows, HEAD_DIM), 1) // 2
    token = (first_token + lax.broadcasted_iota(jnp.int32, (rows, HEAD_DIM), 0)).astype(jnp.float32)
    h_vec = jnp.full((rows, HEAD_DIM), height.astype(jnp.float32))
    w_vec = jnp.full((rows, HEAD_DIM), width.astype(jnp.float32))
    frame = jnp.floor((token + 0.5) / (h_vec * w_vec))
    line = jnp.floor((token + 0.5) / w_vec)
    row = line - h_vec * jnp.floor((line + 0.5) / h_vec)
    col = token - w_vec * line
    position = jnp.where(lanes < time_pairs, frame, jnp.where(lanes < time_pairs + sixth, row, col))
    angles = position * freq
    cos_ref[start : start + rows, :] = jnp.cos(angles)
    sin_ref[start : start + rows, :] = jnp.sin(angles) * sign


def rotate(x, cos, sin, is_even):
    source = x.astype(jnp.float32)
    partner = jnp.where(
        is_even, pltpu.roll(source, HEAD_DIM - 1, 1), pltpu.roll(source, 1, 1)
    )
    return (source * cos + partner * sin).astype(jnp.bfloat16)


def kernel(
    n_seq,
    n_req,
    q_hbm,
    k_hbm,
    v_hbm,
    hidden_hbm,
    w_hbm,
    head_w,
    bias_ref,
    gate_ref,
    mod_ref,
    grid_ref,
    step_ref,
    guide_ref,
    latent_ref,
    next_ref,
    vel_ref,
    q_buf,
    k_buf,
    v_buf,
    hid_buf,
    w_buf,
    att_buf,
    cos_buf,
    sin_buf,
    pred_buf,
    other_buf,
    proj_buf,
    load_sem,
    kv_send,
    kv_recv,
    line_send,
    line_recv,
    x_send,
    x_recv,
    c_send,
    c_recv,
    p_send,
    p_recv,
):
    rows = q_buf.shape[0]
    width = q_buf.shape[1]
    pairs = width // PAIR
    shard = w_hbm.shape[0]
    half = shard // 2
    line_len = n_req // 2
    me_s = lax.axis_index("seq")
    me_c = lax.axis_index("cfg")
    me_r = lax.axis_index("req")
    place = me_r // 2
    x_mate = me_r + 1 - 2 * (me_r % 2)
    other = 1 - me_c

    def remote(src, dst, s_sem, r_sem, **target):
        return pltpu.make_async_remote_copy(
            src_ref=src, dst_ref=dst, send_sem=s_sem, recv_sem=r_sem,
            device_id=target, device_id_type=MESH,
        )

    barrier = pltpu.get_barrier_semaphore()
    for d in range(1, n_seq):
        pl.semaphore_signal(
            barrier, inc=1, device_id={"seq": lax.rem(me_s + d, n_seq)}, device_id_type=MESH
        )
    pl.semaphore_signal(barrier, inc=1, device_id={"cfg": other}, device_id_type=MESH)
    pl.semaphore_signal(barrier, inc=1, device_id={"req": x_mate}, device_id_type=MESH)
    for step in (2, n_req - 2):
        pl.semaphore_signal(
            barrier, inc=1, device_id={"req": lax.rem(me_r + step, n_req)}, device_id_type=MESH
        )

    loads = [
        pltpu.make_async_copy(q_hbm, q_buf, load_sem.at[0]),
        pltpu.make_async_copy(k_hbm, k_buf.at[0:rows, :], load_sem.at[1]),
        pltpu.make_async_copy(v_hbm, v_buf.at[0:rows, :], load_sem.at[2]),
        pltpu.make_async_copy(
            w_hbm, w_buf.at[pl.ds(pl.multiple_of(me_r * shard, shard), shard), :], load_sem.at[3]
        ),
        pltpu.make_async_copy(hidden_hbm, hid_buf, load_sem.at[4]),
    ]
    for load in loads:
        load.start()
    pl.semaphore_wait(barrier, n_seq + 3)

    def kv_copy(d, p, kind):
        cols = slice(p * PAIR, (p + 1) * PAIR)
        src = (k_hbm, v_hbm)[kind].at[:, cols]
        dst = (k_buf, v_buf)[kind].at[d * rows : (d + 1) * rows, cols]
        return remote(
            src, dst, kv_send.at[d - 1, p, kind], kv_recv.at[d - 1, p, kind],
            seq=lax.rem(me_s + d, n_seq),
        )

    kv = {}
    for p in range(pairs):
        for kind in range(2):
            for d in range(1, n_seq):
                kv[d, p, kind] = kv_copy(d, p, kind)

    def piece(owner, which):
        start = pl.multiple_of(owner * shard + which * half, half)
        return w_buf.at[pl.ds(start, half), :]

    own_src = w_hbm.at[pl.ds(pl.multiple_of(me_c * half, half), half), :]

    def toward(side):
        return jnp.maximum(me_r - 2, 0) if side == 0 else jnp.minimum(me_r + 2, n_req - 1)

    def can_pass(side):
        return place >= 1 if side == 0 else place <= line_len - 2

    def comes(side, k):
        return place + k <= line_len - 1 if side == 0 else place - k >= 0

    def owner_of(base, side, k):
        return base + 2 * k if side == 0 else base - 2 * k

    def line_copy(src, owner, side, k):
        return remote(
            src, piece(owner, me_c), line_send.at[side, k], line_recv.at[side, k], req=toward(side)
        )

    def x_copy(src, owner, side, k):
        return remote(src, piece(owner, me_c), x_send.at[side, k], x_recv.at[side, k], req=x_mate)

    def c_copy(owner, which, way, side, k):
        return remote(
            piece(owner, which), piece(owner, which),
            c_send.at[way, side, k], c_recv.at[way, side, k], cfg=other,
        )

    own_x = x_copy(own_src, me_r, 0, 0)
    own_line = [line_copy(own_src, me_r, side, 0) for side in range(2)]
    for d in range(1, n_seq):
        kv[d, 0, 0].start()
        kv[d, 0, 1].start()
    for side in range(2):
        @pl.when(can_pass(side))
        def _():
            own_line[side].start()
    own_x.start()
    for p in range(1, pairs):
        for d in range(1, n_seq):
            kv[d, p, 0].start()
            kv[d, p, 1].start()

    def line_step(k):
        for side in range(2):
            @pl.when(comes(side, k))
            def _():
                owner = owner_of(me_r, side, k)
                line_copy(piece(owner, me_c), owner, side, k - 1).wait_recv()
                if k < line_len - 1:
                    @pl.when(can_pass(side))
                    def _():
                        line_copy(piece(owner, me_c), owner, side, k).start()
                x_copy(piece(owner, me_c), owner, side, k).start()
                c_copy(owner, me_c, 0, side, k).start()

    def x_step(k):
        if k == 0:
            x_copy(own_src, x_mate, 0, 0).wait_recv()
            c_copy(x_mate, me_c, 1, 0, 0).start()
            return
        for side in range(2):
            @pl.when(comes(side, k))
            def _():
                owner = owner_of(x_mate, side, k)
                x_copy(piece(owner, me_c), owner, side, k).wait_recv()
                c_copy(owner, me_c, 1, side, k).start()

    def finish_gather():
        c_copy(x_mate, other, 1, 0, 0).wait_recv()
        for k in range(1, line_len):
            for side in range(2):
                @pl.when(comes(side, k))
                def _():
                    c_copy(owner_of(me_r, side, k), other, 0, side, k).wait_recv()
                    c_copy(owner_of(x_mate, side, k), other, 1, side, k).wait_recv()

    frames, height, across = grid_ref[0, 0], grid_ref[0, 1], grid_ref[0, 2]
    length = frames * height * across
    for d in range(n_seq):
        source = lax.rem(me_s + n_seq - d, n_seq)
        fill_tables(cos_buf, sin_buf, d * rows, rows, source * rows, (height, across))
    total = n_seq * rows
    is_even = lax.broadcasted_iota(jnp.int32, (1, HEAD_DIM), 1) % 2 == 0
    key_slot = lax.broadcasted_iota(jnp.int32, (1, total), 1)
    slot = key_slot // rows
    source = lax.rem(me_s + n_seq - slot, n_seq)
    live_keys = source * rows + key_slot % rows < length
    factor = math.log2(math.e) / math.sqrt(HEAD_DIM)

    loads[0].wait()
    loads[1].wait()
    loads[2].wait()

    def attend_pair(p):
        for d in range(1, n_seq):
            kv[d, p, 0].wait_recv()
            kv[d, p, 1].wait_recv()
        for h in (2 * p, 2 * p + 1):
            cols = slice(h * HEAD_DIM, (h + 1) * HEAD_DIM)
            rot_q = rotate(q_buf[:, cols], cos_buf[0:rows, :], sin_buf[0:rows, :], is_even)
            rot_k = rotate(k_buf[:, cols], cos_buf[...], sin_buf[...], is_even)
            scores = lax.dot_general(
                rot_q, rot_k, (((1,), (1,)), ((), ())), preferred_element_type=jnp.float32
            )
            scores = jnp.where(live_keys, scores, masked_score)
            top = jnp.max(scores, axis=-1, keepdims=True)
            weights = jnp.exp2((scores - top) * factor)
            weight_sum = jnp.sum(weights, axis=-1, keepdims=True)
            mixed = jnp.dot(
                weights.astype(jnp.bfloat16), v_buf[:, cols], preferred_element_type=jnp.float32
            )
            att_buf[:, cols] = (mixed / weight_sum).astype(jnp.bfloat16)

    spread = max(1, -(-(line_len - 1) // max(1, pairs - 1)))
    k = 1
    for p in range(pairs):
        if p < pairs - 1:
            for _ in range(spread):
                if k < line_len:
                    line_step(k)
                    x_step(k - 1)
                    k += 1
        if p == pairs - 1:
            x_step(line_len - 1)
            loads[3].wait()
            loads[4].wait()
            finish_gather()
            done = (pairs - 1) * PAIR
            proj_buf[...] = jnp.dot(
                att_buf[:, 0:done], w_buf[0:done, :], preferred_element_type=jnp.float32
            )
        attend_pair(p)

    last = (pairs - 1) * PAIR
    proj = proj_buf[...] + jnp.dot(
        att_buf[:, last:], w_buf[last:, :], preferred_element_type=jnp.float32
    )
    mixed = hid_buf[...].astype(jnp.float32) + gate_ref[...] * proj
    average = jnp.mean(mixed, axis=-1, keepdims=True)
    centered = mixed - average
    spread_sq = jnp.mean(centered * centered, axis=-1, keepdims=True)
    normed = centered * lax.rsqrt(spread_sq + norm_eps)
    modded = (normed * (1.0 + mod_ref[1:2, :]) + mod_ref[0:1, :]).astype(jnp.bfloat16)
    channels = head_w.shape[0]
    on_diag = lax.broadcasted_iota(jnp.int32, (channels, channels), 0) == lax.broadcasted_iota(
        jnp.int32, (channels, channels), 1
    )
    bias = jnp.sum(jnp.where(on_diag, bias_ref[...], 0.0), axis=1, keepdims=True)
    pred_buf[...] = (
        lax.dot_general(
            head_w[...], modded, (((1,), (1,)), ((), ())), preferred_element_type=jnp.float32
        )
        + bias
    )

    own_width = channels // 2
    swap = remote(
        pred_buf.at[pl.ds(pl.multiple_of(other * own_width, own_width), own_width), :],
        other_buf, p_send, p_recv, cfg=other,
    )
    swap.start()
    own_cols = pred_buf[pl.ds(pl.multiple_of(me_c * own_width, own_width), own_width), :]
    step_vec = jnp.full((own_width, rows), step_ref[0].astype(jnp.float32))
    delta = noise_level(step_vec + 1.0) - noise_level(step_vec)
    live = me_s * rows + lax.broadcasted_iota(jnp.int32, (own_width, rows), 1) < length
    guide = guide_ref[0]

    for copy in kv.values():
        copy.wait_send()
    own_x.wait_send()
    for side in range(2):
        @pl.when(can_pass(side))
        def _():
            own_line[side].wait_send()
    c_copy(x_mate, me_c, 1, 0, 0).wait_send()
    for k in range(1, line_len):
        for side in range(2):
            @pl.when(comes(side, k))
            def _():
                owner = owner_of(me_r, side, k)
                if k < line_len - 1:
                    @pl.when(can_pass(side))
                    def _():
                        line_copy(piece(owner, me_c), owner, side, k).wait_send()
                x_copy(piece(owner, me_c), owner, side, k).wait_send()
                c_copy(owner, me_c, 0, side, k).wait_send()
                c_copy(owner_of(x_mate, side, k), me_c, 1, side, k).wait_send()

    swap.wait()
    other_cols = other_buf[...]
    is_cond = me_c == 0
    cond = jnp.where(is_cond, own_cols, other_cols)
    uncond = jnp.where(is_cond, other_cols, own_cols)
    guided = uncond + guide * (cond - uncond)
    velocity = jnp.where(live, guided, 0.0)
    vel_ref[...] = velocity
    next_ref[...] = latent_ref[...] + delta * velocity


def solution(mesh):
    n_seq, n_req = mesh.shape["seq"], mesh.shape["req"]

    def on_device(
        queries,
        key_vectors,
        values,
        hidden,
        out_proj,
        head_weight,
        head_bias,
        attn_gate,
        shift_scale,
        grid_shape,
        step_index,
        guide_scale,
        latent,
    ):
        rows, width = queries.shape[2:]
        model = hidden.shape[3]
        channels = head_weight.shape[1]
        own_width = latent.shape[2]
        pairs = width // PAIR
        line_len = n_req // 2
        total = n_seq * rows
        any_spec = pl.BlockSpec(memory_space=pl.ANY)
        vmem = pl.BlockSpec(memory_space=pltpu.VMEM)
        smem = pl.BlockSpec(memory_space=pltpu.SMEM)
        dma = pltpu.SemaphoreType.DMA
        out = jax.ShapeDtypeStruct((own_width, rows), jnp.float32)
        next_t, vel_t = pl.pallas_call(
            functools.partial(kernel, n_seq, n_req),
            out_shape=(out, out),
            in_specs=[any_spec] * 5 + [vmem] * 4 + [smem] * 3 + [vmem],
            out_specs=(vmem, vmem),
            scratch_shapes=[
                pltpu.VMEM((rows, width), jnp.bfloat16),
                pltpu.VMEM((total, width), jnp.bfloat16),
                pltpu.VMEM((total, width), jnp.bfloat16),
                pltpu.VMEM((rows, model), jnp.bfloat16),
                pltpu.VMEM((width, model), jnp.bfloat16),
                pltpu.VMEM((rows, width), jnp.bfloat16),
                pltpu.VMEM((total, HEAD_DIM), jnp.float32),
                pltpu.VMEM((total, HEAD_DIM), jnp.float32),
                pltpu.VMEM((channels, rows), jnp.float32),
                pltpu.VMEM((own_width, rows), jnp.float32),
                pltpu.VMEM((rows, model), jnp.float32),
                dma((5,)),
                dma((n_seq - 1, pairs, 2)),
                dma((n_seq - 1, pairs, 2)),
                dma((2, line_len)),
                dma((2, line_len)),
                dma((2, line_len)),
                dma((2, line_len)),
                dma((2, 2, line_len)),
                dma((2, 2, line_len)),
                dma(()),
                dma(()),
            ],
            compiler_params=pltpu.CompilerParams(
                collective_id=0, has_side_effects=True, vmem_limit_bytes=56 * 1024 * 1024
            ),
        )(
            queries[0, 0],
            key_vectors[0, 0],
            values[0, 0],
            hidden[0, 0],
            out_proj,
            head_weight.T,
            head_bias[None, :],
            attn_gate,
            shift_scale[0],
            grid_shape,
            step_index,
            guide_scale,
            latent[0].T,
        )
        return (next_t.T[None], vel_t.T[None])

    return jax.shard_map(
        on_device,
        mesh=mesh,
        in_specs=(
            P("req", "cfg", "seq", None),
            P("req", "cfg", "seq", None),
            P("req", "cfg", "seq", None),
            P("req", "cfg", "seq", None),
            P("req", None),
            P(),
            P(),
            P("req", None),
            P("req", None, None),
            P("req", None),
            P("req"),
            P("req"),
            P("req", "seq", "cfg"),
        ),
        out_specs=(P("req", "seq", "cfg"), P("req", "seq", "cfg")),
        check_vma=False,
    )
```

```python
import functools
import math

import jax
import jax.numpy as jnp
from jax import lax
from jax.experimental import pallas as pl
from jax.experimental.pallas import tpu as pltpu
from jax.sharding import PartitionSpec as P

HEAD_DIM = 128
STEPS = 20
PAIR = 2 * HEAD_DIM

masked_score = -1e30
norm_eps = 1e-06
shift_factor = 5.0
MESH = pl.DeviceIdType.MESH


def noise_level(step_value):
    progress = 1.0 - step_value / STEPS
    return shift_factor * progress / (1.0 + (shift_factor - 1.0) * progress)


def fill_tables(cos_ref, sin_ref, start, rows, first_token, dims):
    height, width = dims
    sixth = HEAD_DIM // 6
    time_pairs = (HEAD_DIM - 4 * sixth) // 2
    lane = lax.broadcasted_iota(jnp.int32, (8, HEAD_DIM), 1)
    pair = lane // 2
    is_time = pair < time_pairs
    is_row = pair < time_pairs + sixth
    pair_f = pair.astype(jnp.float32)
    space = pair_f - time_pairs
    exponent = jnp.where(
        is_time, pair_f / time_pairs, jnp.where(is_row, space / sixth, (space - sixth) / sixth)
    )
    freq = jnp.exp(exponent * -math.log(10000.0))[0:1]
    sign = jnp.where(lane % 2 == 0, -1.0, 1.0).astype(jnp.float32)[0:1]
    lanes = lax.broadcasted_iota(jnp.int32, (rows, HEAD_DIM), 1) // 2
    token = (first_token + lax.broadcasted_iota(jnp.int32, (rows, HEAD_DIM), 0)).astype(jnp.float32)
    h_vec = jnp.full((rows, HEAD_DIM), height.astype(jnp.float32))
    w_vec = jnp.full((rows, HEAD_DIM), width.astype(jnp.float32))
    frame = jnp.floor((token + 0.5) / (h_vec * w_vec))
    line = jnp.floor((token + 0.5) / w_vec)
    row = line - h_vec * jnp.floor((line + 0.5) / h_vec)
    col = token - w_vec * line
    position = jnp.where(lanes < time_pairs, frame, jnp.where(lanes < time_pairs + sixth, row, col))
    angles = position * freq
    cos_ref[start : start + rows, :] = jnp.cos(angles)
    sin_ref[start : start + rows, :] = jnp.sin(angles) * sign


def rotate(x, cos, sin, is_even):
    source = x.astype(jnp.float32)
    partner = jnp.where(
        is_even, pltpu.roll(source, HEAD_DIM - 1, 1), pltpu.roll(source, 1, 1)
    )
    return (source * cos + partner * sin).astype(jnp.bfloat16)


def kernel(
    n_seq,
    n_req,
    q_hbm,
    k_hbm,
    v_hbm,
    hidden_hbm,
    w_hbm,
    head_w_hbm,
    bias_hbm,
    gate_hbm,
    mod_hbm,
    grid_hbm,
    step_hbm,
    guide_hbm,
    out_ref,
    q_buf,
    k_buf,
    v_buf,
    hid_buf,
    w_buf,
    att_buf,
    cos_buf,
    sin_buf,
    pred_buf,
    other_buf,
    proj_buf,
    head_w,
    bias_ref,
    gate_ref,
    mod_ref,
    grid_ref,
    step_ref,
    guide_ref,
    load_sem,
    kv_send,
    kv_recv,
    line_send,
    line_recv,
    x_send,
    x_recv,
    c_send,
    c_recv,
    p_send,
    p_recv,
):
    rows = q_buf.shape[0]
    width = q_buf.shape[1]
    pairs = width // PAIR
    shard = w_hbm.shape[0]
    half = shard // 2
    line_len = n_req // 2
    me_s = lax.axis_index("seq")
    me_c = lax.axis_index("cfg")
    me_r = lax.axis_index("req")
    place = me_r // 2
    x_mate = me_r + 1 - 2 * (me_r % 2)
    other = 1 - me_c

    def remote(src, dst, s_sem, r_sem, **target):
        return pltpu.make_async_remote_copy(
            src_ref=src, dst_ref=dst, send_sem=s_sem, recv_sem=r_sem,
            device_id=target, device_id_type=MESH,
        )

    barrier = pltpu.get_barrier_semaphore()
    for d in range(1, n_seq):
        pl.semaphore_signal(
            barrier, inc=1, device_id={"seq": lax.rem(me_s + d, n_seq)}, device_id_type=MESH
        )
    pl.semaphore_signal(barrier, inc=1, device_id={"cfg": other}, device_id_type=MESH)
    pl.semaphore_signal(barrier, inc=1, device_id={"req": x_mate}, device_id_type=MESH)
    for step in (2, n_req - 2):
        pl.semaphore_signal(
            barrier, inc=1, device_id={"req": lax.rem(me_r + step, n_req)}, device_id_type=MESH
        )

    loads = [
        pltpu.make_async_copy(q_hbm, q_buf, load_sem.at[0]),
        pltpu.make_async_copy(k_hbm, k_buf.at[0:rows, :], load_sem.at[1]),
        pltpu.make_async_copy(v_hbm, v_buf.at[0:rows, :], load_sem.at[2]),
        pltpu.make_async_copy(
            w_hbm, w_buf.at[pl.ds(pl.multiple_of(me_r * shard, shard), shard), :], load_sem.at[3]
        ),
        pltpu.make_async_copy(hidden_hbm, hid_buf, load_sem.at[4]),
        pltpu.make_async_copy(grid_hbm, grid_ref, load_sem.at[5]),
        pltpu.make_async_copy(step_hbm, step_ref, load_sem.at[6]),
        pltpu.make_async_copy(guide_hbm, guide_ref, load_sem.at[7]),
        pltpu.make_async_copy(head_w_hbm, head_w, load_sem.at[8]),
        pltpu.make_async_copy(bias_hbm, bias_ref, load_sem.at[9]),
        pltpu.make_async_copy(gate_hbm, gate_ref, load_sem.at[10]),
        pltpu.make_async_copy(mod_hbm, mod_ref, load_sem.at[11]),
    ]
    for load in loads:
        load.start()
    pl.semaphore_wait(barrier, n_seq + 3)

    def kv_copy(d, p, kind):
        cols = slice(p * PAIR, (p + 1) * PAIR)
        src = (k_hbm, v_hbm)[kind].at[:, cols]
        dst = (k_buf, v_buf)[kind].at[d * rows : (d + 1) * rows, cols]
        return remote(
            src, dst, kv_send.at[d - 1, p, kind], kv_recv.at[d - 1, p, kind],
            seq=lax.rem(me_s + d, n_seq),
        )

    kv = {}
    for p in range(pairs):
        for kind in range(2):
            for d in range(1, n_seq):
                kv[d, p, kind] = kv_copy(d, p, kind)

    def piece(owner, which):
        start = pl.multiple_of(owner * shard + which * half, half)
        return w_buf.at[pl.ds(start, half), :]

    own_src = w_hbm.at[pl.ds(pl.multiple_of(me_c * half, half), half), :]

    def toward(side):
        return jnp.maximum(me_r - 2, 0) if side == 0 else jnp.minimum(me_r + 2, n_req - 1)

    def can_pass(side):
        return place >= 1 if side == 0 else place <= line_len - 2

    def comes(side, k):
        return place + k <= line_len - 1 if side == 0 else place - k >= 0

    def owner_of(base, side, k):
        return base + 2 * k if side == 0 else base - 2 * k

    def line_copy(src, owner, side, k):
        return remote(
            src, piece(owner, me_c), line_send.at[side, k], line_recv.at[side, k], req=toward(side)
        )

    def x_copy(src, owner, side, k):
        return remote(src, piece(owner, me_c), x_send.at[side, k], x_recv.at[side, k], req=x_mate)

    def c_copy(owner, which, way, side, k):
        return remote(
            piece(owner, which), piece(owner, which),
            c_send.at[way, side, k], c_recv.at[way, side, k], cfg=other,
        )

    own_x = x_copy(own_src, me_r, 0, 0)
    own_line = [line_copy(own_src, me_r, side, 0) for side in range(2)]
    for d in range(1, n_seq):
        kv[d, 0, 0].start()
        kv[d, 0, 1].start()
    for side in range(2):
        @pl.when(can_pass(side))
        def _():
            own_line[side].start()
    own_x.start()
    for p in range(1, pairs):
        for d in range(1, n_seq):
            kv[d, p, 0].start()
            kv[d, p, 1].start()

    def line_step(k):
        for side in range(2):
            @pl.when(comes(side, k))
            def _():
                owner = owner_of(me_r, side, k)
                line_copy(piece(owner, me_c), owner, side, k - 1).wait_recv()
                if k < line_len - 1:
                    @pl.when(can_pass(side))
                    def _():
                        line_copy(piece(owner, me_c), owner, side, k).start()
                x_copy(piece(owner, me_c), owner, side, k).start()
                c_copy(owner, me_c, 0, side, k).start()

    def x_step(k):
        if k == 0:
            x_copy(own_src, x_mate, 0, 0).wait_recv()
            c_copy(x_mate, me_c, 1, 0, 0).start()
            return
        for side in range(2):
            @pl.when(comes(side, k))
            def _():
                owner = owner_of(x_mate, side, k)
                x_copy(piece(owner, me_c), owner, side, k).wait_recv()
                c_copy(owner, me_c, 1, side, k).start()

    def finish_gather():
        c_copy(x_mate, other, 1, 0, 0).wait_recv()
        for k in range(1, line_len):
            for side in range(2):
                @pl.when(comes(side, k))
                def _():
                    c_copy(owner_of(me_r, side, k), other, 0, side, k).wait_recv()
                    c_copy(owner_of(x_mate, side, k), other, 1, side, k).wait_recv()

    loads[5].wait()
    frames, height, across = grid_ref[0, 0], grid_ref[0, 1], grid_ref[0, 2]
    length = frames * height * across
    for d in range(n_seq):
        source = lax.rem(me_s + n_seq - d, n_seq)
        fill_tables(cos_buf, sin_buf, d * rows, rows, source * rows, (height, across))
    total = n_seq * rows
    is_even = lax.broadcasted_iota(jnp.int32, (1, HEAD_DIM), 1) % 2 == 0
    key_slot = lax.broadcasted_iota(jnp.int32, (1, total), 1)
    slot = key_slot // rows
    source = lax.rem(me_s + n_seq - slot, n_seq)
    live_keys = source * rows + key_slot % rows < length
    factor = math.log2(math.e) / math.sqrt(HEAD_DIM)

    loads[0].wait()
    loads[1].wait()
    loads[2].wait()

    def attend_pair(p):
        heads = [slice(h * HEAD_DIM, (h + 1) * HEAD_DIM) for h in (2 * p, 2 * p + 1)]
        for d in range(1, n_seq):
            kv[d, p, 0].wait_recv()
        staged = []
        for cols in heads:
            rot_q = rotate(q_buf[:, cols], cos_buf[0:rows, :], sin_buf[0:rows, :], is_even)
            rot_k = rotate(k_buf[:, cols], cos_buf[...], sin_buf[...], is_even)
            scores = lax.dot_general(
                rot_q, rot_k, (((1,), (1,)), ((), ())), preferred_element_type=jnp.float32
            )
            scores = jnp.where(live_keys, scores, masked_score)
            top = jnp.max(scores, axis=-1, keepdims=True)
            weights = jnp.exp2((scores - top) * factor)
            weight_sum = jnp.sum(weights, axis=-1, keepdims=True)
            staged.append((weights.astype(jnp.bfloat16), weight_sum))
        for d in range(1, n_seq):
            kv[d, p, 1].wait_recv()
        for cols, (weights, weight_sum) in zip(heads, staged):
            mixed = jnp.dot(weights, v_buf[:, cols], preferred_element_type=jnp.float32)
            att_buf[:, cols] = (mixed / weight_sum).astype(jnp.bfloat16)

    spread = max(1, -(-(line_len - 1) // max(1, pairs - 1)))
    k = 1
    for p in range(pairs):
        if p < pairs - 1:
            for _ in range(spread):
                if k < line_len:
                    line_step(k)
                    x_step(k - 1)
                    k += 1
        if p == pairs - 1:
            x_step(line_len - 1)
            loads[3].wait()
            loads[4].wait()
            for load in loads[6:]:
                load.wait()
            finish_gather()
            done = (pairs - 1) * PAIR
            proj_buf[...] = jnp.dot(
                att_buf[:, 0:done], w_buf[0:done, :], preferred_element_type=jnp.float32
            )
        attend_pair(p)

    last = (pairs - 1) * PAIR
    proj = proj_buf[...] + jnp.dot(
        att_buf[:, last:], w_buf[last:, :], preferred_element_type=jnp.float32
    )
    mixed = hid_buf[...].astype(jnp.float32) + gate_ref[...] * proj
    average = jnp.mean(mixed, axis=-1, keepdims=True)
    centered = mixed - average
    spread_sq = jnp.mean(centered * centered, axis=-1, keepdims=True)
    normed = centered * lax.rsqrt(spread_sq + norm_eps)
    modded = (normed * (1.0 + mod_ref[1:2, :]) + mod_ref[0:1, :]).astype(jnp.bfloat16)
    channels = head_w.shape[0]
    on_diag = lax.broadcasted_iota(jnp.int32, (channels, channels), 0) == lax.broadcasted_iota(
        jnp.int32, (channels, channels), 1
    )
    bias = jnp.sum(jnp.where(on_diag, bias_ref[...], 0.0), axis=1, keepdims=True)
    pred_buf[...] = (
        lax.dot_general(
            head_w[...], modded, (((1,), (1,)), ((), ())), preferred_element_type=jnp.float32
        )
        + bias
    )

    own_width = channels // 2
    swap = remote(
        pred_buf.at[pl.ds(pl.multiple_of(other * own_width, own_width), own_width), :],
        other_buf, p_send, p_recv, cfg=other,
    )
    swap.start()
    own_cols = pred_buf[pl.ds(pl.multiple_of(me_c * own_width, own_width), own_width), :]
    step_vec = jnp.full((own_width, rows), step_ref[0].astype(jnp.float32))
    delta = noise_level(step_vec + 1.0) - noise_level(step_vec)
    live = me_s * rows + lax.broadcasted_iota(jnp.int32, (own_width, rows), 1) < length
    guide = guide_ref[0]

    for copy in kv.values():
        copy.wait_send()
    own_x.wait_send()
    for side in range(2):
        @pl.when(can_pass(side))
        def _():
            own_line[side].wait_send()
    c_copy(x_mate, me_c, 1, 0, 0).wait_send()
    for k in range(1, line_len):
        for side in range(2):
            @pl.when(comes(side, k))
            def _():
                owner = owner_of(me_r, side, k)
                if k < line_len - 1:
                    @pl.when(can_pass(side))
                    def _():
                        line_copy(piece(owner, me_c), owner, side, k).wait_send()
                x_copy(piece(owner, me_c), owner, side, k).wait_send()
                c_copy(owner, me_c, 0, side, k).wait_send()
                c_copy(owner_of(x_mate, side, k), me_c, 1, side, k).wait_send()

    swap.wait()
    other_cols = other_buf[...]
    is_cond = me_c == 0
    cond = jnp.where(is_cond, own_cols, other_cols)
    uncond = jnp.where(is_cond, other_cols, own_cols)
    guided = uncond + guide * (cond - uncond)
    velocity = jnp.where(live, guided, 0.0)
    out_ref[0:own_width, :] = velocity
    out_ref[own_width:, :] = delta * velocity


def solution(mesh):
    n_seq, n_req = mesh.shape["seq"], mesh.shape["req"]

    def on_device(
        queries,
        key_vectors,
        values,
        hidden,
        out_proj,
        head_weight,
        head_bias,
        attn_gate,
        shift_scale,
        grid_shape,
        step_index,
        guide_scale,
        latent,
    ):
        rows, width = queries.shape[2:]
        model = hidden.shape[3]
        channels = head_weight.shape[1]
        own_width = latent.shape[2]
        pairs = width // PAIR
        line_len = n_req // 2
        total = n_seq * rows
        any_spec = pl.BlockSpec(memory_space=pl.ANY)
        dma = pltpu.SemaphoreType.DMA
        out = pl.pallas_call(
            functools.partial(kernel, n_seq, n_req),
            out_shape=jax.ShapeDtypeStruct((2 * own_width, rows), jnp.float32),
            in_specs=[any_spec] * 12,
            out_specs=pl.BlockSpec(memory_space=pltpu.VMEM),
            scratch_shapes=[
                pltpu.VMEM((rows, width), jnp.bfloat16),
                pltpu.VMEM((total, width), jnp.bfloat16),
                pltpu.VMEM((total, width), jnp.bfloat16),
                pltpu.VMEM((rows, model), jnp.bfloat16),
                pltpu.VMEM((width, model), jnp.bfloat16),
                pltpu.VMEM((rows, width), jnp.bfloat16),
                pltpu.VMEM((total, HEAD_DIM), jnp.float32),
                pltpu.VMEM((total, HEAD_DIM), jnp.float32),
                pltpu.VMEM((channels, rows), jnp.float32),
                pltpu.VMEM((own_width, rows), jnp.float32),
                pltpu.VMEM((rows, model), jnp.float32),
                pltpu.VMEM((channels, model), jnp.bfloat16),
                pltpu.VMEM((1, channels), jnp.float32),
                pltpu.VMEM((1, model), jnp.float32),
                pltpu.VMEM((2, model), jnp.float32),
                pltpu.SMEM((1, 3), jnp.int32),
                pltpu.SMEM((1,), jnp.int32),
                pltpu.SMEM((1,), jnp.float32),
                dma((12,)),
                dma((n_seq - 1, pairs, 2)),
                dma((n_seq - 1, pairs, 2)),
                dma((2, line_len)),
                dma((2, line_len)),
                dma((2, line_len)),
                dma((2, line_len)),
                dma((2, 2, line_len)),
                dma((2, 2, line_len)),
                dma(()),
                dma(()),
            ],
            compiler_params=pltpu.CompilerParams(
                collective_id=0, has_side_effects=True, vmem_limit_bytes=56 * 1024 * 1024
            ),
        )(
            queries[0, 0],
            key_vectors[0, 0],
            values[0, 0],
            hidden[0, 0],
            out_proj,
            head_weight.T,
            head_bias[None, :],
            attn_gate,
            shift_scale[0],
            grid_shape,
            step_index,
            guide_scale,
        )
        velocity = out[0:own_width].T[None]
        return (latent + out[own_width:].T[None], velocity)

    return jax.shard_map(
        on_device,
        mesh=mesh,
        in_specs=(
            P("req", "cfg", "seq", None),
            P("req", "cfg", "seq", None),
            P("req", "cfg", "seq", None),
            P("req", "cfg", "seq", None),
            P("req", None),
            P(),
            P(),
            P("req", None),
            P("req", None, None),
            P("req", None),
            P("req"),
            P("req"),
            P("req", "seq", "cfg"),
        ),
        out_specs=(P("req", "seq", "cfg"), P("req", "seq", "cfg")),
        check_vma=False,
    )
```

```python
import functools
import math

import jax
import jax.numpy as jnp
from jax import lax
from jax.experimental import pallas as pl
from jax.experimental.pallas import tpu as pltpu
from jax.sharding import PartitionSpec as P

HEAD_DIM = 128
STEPS = 20
PAIR = 2 * HEAD_DIM

masked_score = -1e30
norm_eps = 1e-06
shift_factor = 5.0
MESH = pl.DeviceIdType.MESH


def noise_level(step_value):
    progress = 1.0 - step_value / STEPS
    return shift_factor * progress / (1.0 + (shift_factor - 1.0) * progress)


def fill_tables(cos_ref, sin_ref, start, rows, first_token, dims):
    height, width = dims
    sixth = HEAD_DIM // 6
    time_pairs = (HEAD_DIM - 4 * sixth) // 2
    lane = lax.broadcasted_iota(jnp.int32, (8, HEAD_DIM), 1)
    pair = lane // 2
    is_time = pair < time_pairs
    is_row = pair < time_pairs + sixth
    pair_f = pair.astype(jnp.float32)
    space = pair_f - time_pairs
    exponent = jnp.where(
        is_time, pair_f / time_pairs, jnp.where(is_row, space / sixth, (space - sixth) / sixth)
    )
    freq = jnp.exp(exponent * -math.log(10000.0))[0:1]
    sign = jnp.where(lane % 2 == 0, -1.0, 1.0).astype(jnp.float32)[0:1]
    lanes = lax.broadcasted_iota(jnp.int32, (rows, HEAD_DIM), 1) // 2
    token = (first_token + lax.broadcasted_iota(jnp.int32, (rows, HEAD_DIM), 0)).astype(jnp.float32)
    h_vec = jnp.full((rows, HEAD_DIM), height.astype(jnp.float32))
    w_vec = jnp.full((rows, HEAD_DIM), width.astype(jnp.float32))
    frame = jnp.floor((token + 0.5) / (h_vec * w_vec))
    line = jnp.floor((token + 0.5) / w_vec)
    row = line - h_vec * jnp.floor((line + 0.5) / h_vec)
    col = token - w_vec * line
    position = jnp.where(lanes < time_pairs, frame, jnp.where(lanes < time_pairs + sixth, row, col))
    angles = position * freq
    cos_ref[start : start + rows, :] = jnp.cos(angles)
    sin_ref[start : start + rows, :] = jnp.sin(angles) * sign


def rotate(x, cos, sin, is_even):
    source = x.astype(jnp.float32)
    partner = jnp.where(
        is_even, pltpu.roll(source, HEAD_DIM - 1, 1), pltpu.roll(source, 1, 1)
    )
    return (source * cos + partner * sin).astype(jnp.bfloat16)


def kernel(
    n_seq,
    n_req,
    q_hbm,
    k_hbm,
    v_hbm,
    hidden_hbm,
    w_hbm,
    head_w_hbm,
    bias_hbm,
    gate_hbm,
    mod_hbm,
    grid_hbm,
    step_hbm,
    guide_hbm,
    out_ref,
    q_buf,
    k_buf,
    v_buf,
    hid_buf,
    w_buf,
    att_buf,
    cos_buf,
    sin_buf,
    pred_buf,
    other_buf,
    proj_buf,
    head_w,
    bias_ref,
    gate_ref,
    mod_ref,
    grid_ref,
    step_ref,
    guide_ref,
    load_sem,
    kv_send,
    kv_recv,
    line_send,
    line_recv,
    x_send,
    x_recv,
    c_send,
    c_recv,
    p_send,
    p_recv,
):
    rows = q_buf.shape[0]
    width = q_buf.shape[1]
    pairs = width // PAIR
    shard = w_hbm.shape[0]
    half = shard // 2
    line_len = n_req // 2
    me_s = lax.axis_index("seq")
    me_c = lax.axis_index("cfg")
    me_r = lax.axis_index("req")
    place = me_r // 2
    x_mate = me_r + 1 - 2 * (me_r % 2)
    other = 1 - me_c

    def remote(src, dst, s_sem, r_sem, **target):
        return pltpu.make_async_remote_copy(
            src_ref=src, dst_ref=dst, send_sem=s_sem, recv_sem=r_sem,
            device_id=target, device_id_type=MESH,
        )

    barrier = pltpu.get_barrier_semaphore()
    for d in range(1, n_seq):
        pl.semaphore_signal(
            barrier, inc=1, device_id={"seq": lax.rem(me_s + d, n_seq)}, device_id_type=MESH
        )
    pl.semaphore_signal(barrier, inc=1, device_id={"cfg": other}, device_id_type=MESH)
    pl.semaphore_signal(barrier, inc=1, device_id={"req": x_mate}, device_id_type=MESH)
    for step in (2, n_req - 2):
        pl.semaphore_signal(
            barrier, inc=1, device_id={"req": lax.rem(me_r + step, n_req)}, device_id_type=MESH
        )

    loads = [
        pltpu.make_async_copy(q_hbm, q_buf, load_sem.at[0]),
        pltpu.make_async_copy(k_hbm, k_buf.at[0:rows, :], load_sem.at[1]),
        pltpu.make_async_copy(v_hbm, v_buf.at[0:rows, :], load_sem.at[2]),
        pltpu.make_async_copy(
            w_hbm, w_buf.at[pl.ds(pl.multiple_of(me_r * shard, shard), shard), :], load_sem.at[3]
        ),
        pltpu.make_async_copy(hidden_hbm, hid_buf, load_sem.at[4]),
        pltpu.make_async_copy(grid_hbm, grid_ref, load_sem.at[5]),
        pltpu.make_async_copy(step_hbm, step_ref, load_sem.at[6]),
        pltpu.make_async_copy(guide_hbm, guide_ref, load_sem.at[7]),
        pltpu.make_async_copy(head_w_hbm, head_w, load_sem.at[8]),
        pltpu.make_async_copy(bias_hbm, bias_ref, load_sem.at[9]),
        pltpu.make_async_copy(gate_hbm, gate_ref, load_sem.at[10]),
        pltpu.make_async_copy(mod_hbm, mod_ref, load_sem.at[11]),
    ]
    for i in (1, 2, 0, *range(3, len(loads))):
        loads[i].start()
    loads[1].wait()
    loads[2].wait()
    pl.semaphore_wait(barrier, n_seq + 3)

    def kv_copy(d, p, kind):
        cols = slice(p * PAIR, (p + 1) * PAIR)
        src = (k_buf, v_buf)[kind].at[0:rows, cols]
        dst = (k_buf, v_buf)[kind].at[d * rows : (d + 1) * rows, cols]
        return remote(
            src, dst, kv_send.at[d - 1, p, kind], kv_recv.at[d - 1, p, kind],
            seq=lax.rem(me_s + d, n_seq),
        )

    kv = {}
    for p in range(pairs):
        for kind in range(2):
            for d in range(1, n_seq):
                kv[d, p, kind] = kv_copy(d, p, kind)

    def piece(owner, which):
        start = pl.multiple_of(owner * shard + which * half, half)
        return w_buf.at[pl.ds(start, half), :]

    own_src = w_hbm.at[pl.ds(pl.multiple_of(me_c * half, half), half), :]

    def toward(side):
        return jnp.maximum(me_r - 2, 0) if side == 0 else jnp.minimum(me_r + 2, n_req - 1)

    def can_pass(side):
        return place >= 1 if side == 0 else place <= line_len - 2

    def comes(side, k):
        return place + k <= line_len - 1 if side == 0 else place - k >= 0

    def owner_of(base, side, k):
        return base + 2 * k if side == 0 else base - 2 * k

    def line_copy(src, owner, side, k):
        return remote(
            src, piece(owner, me_c), line_send.at[side, k], line_recv.at[side, k], req=toward(side)
        )

    def x_copy(src, owner, side, k):
        return remote(src, piece(owner, me_c), x_send.at[side, k], x_recv.at[side, k], req=x_mate)

    def c_copy(owner, which, way, side, k):
        return remote(
            piece(owner, which), piece(owner, which),
            c_send.at[way, side, k], c_recv.at[way, side, k], cfg=other,
        )

    own_x = x_copy(own_src, me_r, 0, 0)
    own_line = [line_copy(own_src, me_r, side, 0) for side in range(2)]
    for d in range(1, n_seq):
        kv[d, 0, 0].start()
        kv[d, 0, 1].start()
    for side in range(2):
        @pl.when(can_pass(side))
        def _():
            own_line[side].start()
    own_x.start()
    for p in range(1, pairs):
        for d in range(1, n_seq):
            kv[d, p, 0].start()
            kv[d, p, 1].start()

    def line_step(k):
        for side in range(2):
            @pl.when(comes(side, k))
            def _():
                owner = owner_of(me_r, side, k)
                line_copy(piece(owner, me_c), owner, side, k - 1).wait_recv()
                if k < line_len - 1:
                    @pl.when(can_pass(side))
                    def _():
                        line_copy(piece(owner, me_c), owner, side, k).start()
                x_copy(piece(owner, me_c), owner, side, k).start()
                c_copy(owner, me_c, 0, side, k).start()

    def x_step(k):
        if k == 0:
            x_copy(own_src, x_mate, 0, 0).wait_recv()
            c_copy(x_mate, me_c, 1, 0, 0).start()
            return
        for side in range(2):
            @pl.when(comes(side, k))
            def _():
                owner = owner_of(x_mate, side, k)
                x_copy(piece(owner, me_c), owner, side, k).wait_recv()
                c_copy(owner, me_c, 1, side, k).start()

    def finish_gather():
        c_copy(x_mate, other, 1, 0, 0).wait_recv()
        for k in range(1, line_len):
            for side in range(2):
                @pl.when(comes(side, k))
                def _():
                    c_copy(owner_of(me_r, side, k), other, 0, side, k).wait_recv()
                    c_copy(owner_of(x_mate, side, k), other, 1, side, k).wait_recv()

    loads[5].wait()
    frames, height, across = grid_ref[0, 0], grid_ref[0, 1], grid_ref[0, 2]
    length = frames * height * across
    for d in range(n_seq):
        source = lax.rem(me_s + n_seq - d, n_seq)
        fill_tables(cos_buf, sin_buf, d * rows, rows, source * rows, (height, across))
    total = n_seq * rows
    is_even = lax.broadcasted_iota(jnp.int32, (1, HEAD_DIM), 1) % 2 == 0
    key_slot = lax.broadcasted_iota(jnp.int32, (1, total), 1)
    slot = key_slot // rows
    source = lax.rem(me_s + n_seq - slot, n_seq)
    live_keys = source * rows + key_slot % rows < length
    factor = math.log2(math.e) / math.sqrt(HEAD_DIM)

    loads[0].wait()

    def attend_pair(p):
        heads = [slice(h * HEAD_DIM, (h + 1) * HEAD_DIM) for h in (2 * p, 2 * p + 1)]
        for d in range(1, n_seq):
            kv[d, p, 0].wait_recv()
        staged = []
        for cols in heads:
            rot_q = rotate(q_buf[:, cols], cos_buf[0:rows, :], sin_buf[0:rows, :], is_even)
            rot_k = rotate(k_buf[:, cols], cos_buf[...], sin_buf[...], is_even)
            scores = lax.dot_general(
                rot_q, rot_k, (((1,), (1,)), ((), ())), preferred_element_type=jnp.float32
            )
            scores = jnp.where(live_keys, scores, masked_score)
            top = jnp.max(scores, axis=-1, keepdims=True)
            weights = jnp.exp2((scores - top) * factor)
            weight_sum = jnp.sum(weights, axis=-1, keepdims=True)
            staged.append((weights.astype(jnp.bfloat16), weight_sum))
        for d in range(1, n_seq):
            kv[d, p, 1].wait_recv()
        for cols, (weights, weight_sum) in zip(heads, staged):
            mixed = jnp.dot(weights, v_buf[:, cols], preferred_element_type=jnp.float32)
            att_buf[:, cols] = (mixed / weight_sum).astype(jnp.bfloat16)

    spread = max(1, -(-(line_len - 1) // max(1, pairs - 1)))
    k = 1
    for p in range(pairs):
        if p < pairs - 1:
            for _ in range(spread):
                if k < line_len:
                    line_step(k)
                    x_step(k - 1)
                    k += 1
        if p == pairs - 1:
            x_step(line_len - 1)
            loads[3].wait()
            loads[4].wait()
            for load in loads[6:]:
                load.wait()
            finish_gather()
            done = (pairs - 1) * PAIR
            proj_buf[...] = hid_buf[...].astype(jnp.float32) + gate_ref[...] * jnp.dot(
                att_buf[:, 0:done], w_buf[0:done, :], preferred_element_type=jnp.float32
            )
        attend_pair(p)

    last = (pairs - 1) * PAIR
    mixed = proj_buf[...] + gate_ref[...] * jnp.dot(
        att_buf[:, last:], w_buf[last:, :], preferred_element_type=jnp.float32
    )
    average = jnp.mean(mixed, axis=-1, keepdims=True)
    centered = mixed - average
    spread_sq = jnp.mean(centered * centered, axis=-1, keepdims=True)
    normed = centered * lax.rsqrt(spread_sq + norm_eps)
    modded = (normed * (1.0 + mod_ref[1:2, :]) + mod_ref[0:1, :]).astype(jnp.bfloat16)
    channels = head_w.shape[0]
    on_diag = lax.broadcasted_iota(jnp.int32, (channels, channels), 0) == lax.broadcasted_iota(
        jnp.int32, (channels, channels), 1
    )
    bias = jnp.sum(jnp.where(on_diag, bias_ref[...], 0.0), axis=1, keepdims=True)
    pred_buf[...] = (
        lax.dot_general(
            head_w[...], modded, (((1,), (1,)), ((), ())), preferred_element_type=jnp.float32
        )
        + bias
    )

    own_width = channels // 2
    swap = remote(
        pred_buf.at[pl.ds(pl.multiple_of(other * own_width, own_width), own_width), :],
        other_buf, p_send, p_recv, cfg=other,
    )
    swap.start()
    own_cols = pred_buf[pl.ds(pl.multiple_of(me_c * own_width, own_width), own_width), :]
    step_vec = jnp.full((8, rows), step_ref[0].astype(jnp.float32))
    delta = noise_level(step_vec + 1.0) - noise_level(step_vec)
    live = me_s * rows + lax.broadcasted_iota(jnp.int32, (own_width, rows), 1) < length
    guide = guide_ref[0]

    for copy in kv.values():
        copy.wait_send()
    own_x.wait_send()
    for side in range(2):
        @pl.when(can_pass(side))
        def _():
            own_line[side].wait_send()
    c_copy(x_mate, me_c, 1, 0, 0).wait_send()
    for k in range(1, line_len):
        for side in range(2):
            @pl.when(comes(side, k))
            def _():
                owner = owner_of(me_r, side, k)
                if k < line_len - 1:
                    @pl.when(can_pass(side))
                    def _():
                        line_copy(piece(owner, me_c), owner, side, k).wait_send()
                x_copy(piece(owner, me_c), owner, side, k).wait_send()
                c_copy(owner, me_c, 0, side, k).wait_send()
                c_copy(owner_of(x_mate, side, k), me_c, 1, side, k).wait_send()

    swap.wait()
    other_cols = other_buf[...]
    is_cond = me_c == 0
    cond = jnp.where(is_cond, own_cols, other_cols)
    uncond = jnp.where(is_cond, other_cols, own_cols)
    out_ref[0:own_width, :] = jnp.where(live, uncond, 0.0)
    out_ref[own_width : 2 * own_width, :] = jnp.where(live, guide * (cond - uncond), 0.0)
    out_ref[2 * own_width :, :] = delta


def solution(mesh):
    n_seq, n_req = mesh.shape["seq"], mesh.shape["req"]

    def on_device(
        queries,
        key_vectors,
        values,
        hidden,
        out_proj,
        head_weight,
        head_bias,
        attn_gate,
        shift_scale,
        grid_shape,
        step_index,
        guide_scale,
        latent,
    ):
        rows, width = queries.shape[2:]
        model = hidden.shape[3]
        channels = head_weight.shape[1]
        own_width = latent.shape[2]
        pairs = width // PAIR
        line_len = n_req // 2
        total = n_seq * rows
        any_spec = pl.BlockSpec(memory_space=pl.ANY)
        dma = pltpu.SemaphoreType.DMA
        out = pl.pallas_call(
            functools.partial(kernel, n_seq, n_req),
            out_shape=jax.ShapeDtypeStruct((2 * own_width + 8, rows), jnp.float32),
            in_specs=[any_spec] * 12,
            out_specs=pl.BlockSpec(memory_space=pltpu.VMEM),
            scratch_shapes=[
                pltpu.VMEM((rows, width), jnp.bfloat16),
                pltpu.VMEM((total, width), jnp.bfloat16),
                pltpu.VMEM((total, width), jnp.bfloat16),
                pltpu.VMEM((rows, model), jnp.bfloat16),
                pltpu.VMEM((width, model), jnp.bfloat16),
                pltpu.VMEM((rows, width), jnp.bfloat16),
                pltpu.VMEM((total, HEAD_DIM), jnp.float32),
                pltpu.VMEM((total, HEAD_DIM), jnp.float32),
                pltpu.VMEM((channels, rows), jnp.float32),
                pltpu.VMEM((own_width, rows), jnp.float32),
                pltpu.VMEM((rows, model), jnp.float32),
                pltpu.VMEM((channels, model), jnp.bfloat16),
                pltpu.VMEM((1, channels), jnp.float32),
                pltpu.VMEM((1, model), jnp.float32),
                pltpu.VMEM((2, model), jnp.float32),
                pltpu.SMEM((1, 3), jnp.int32),
                pltpu.SMEM((1,), jnp.int32),
                pltpu.SMEM((1,), jnp.float32),
                dma((12,)),
                dma((n_seq - 1, pairs, 2)),
                dma((n_seq - 1, pairs, 2)),
                dma((2, line_len)),
                dma((2, line_len)),
                dma((2, line_len)),
                dma((2, line_len)),
                dma((2, 2, line_len)),
                dma((2, 2, line_len)),
                dma(()),
                dma(()),
            ],
            compiler_params=pltpu.CompilerParams(
                collective_id=0, has_side_effects=True, vmem_limit_bytes=56 * 1024 * 1024
            ),
        )(
            queries[0, 0],
            key_vectors[0, 0],
            values[0, 0],
            hidden[0, 0],
            out_proj,
            head_weight.T,
            head_bias[None, :],
            attn_gate,
            shift_scale[0],
            grid_shape,
            step_index,
            guide_scale,
        )
        velocity = out[0:own_width] + out[own_width : 2 * own_width]
        next_latent = latent[0].T + out[2 * own_width : 2 * own_width + 1] * velocity
        return (next_latent.T[None], velocity.T[None])

    return jax.shard_map(
        on_device,
        mesh=mesh,
        in_specs=(
            P("req", "cfg", "seq", None),
            P("req", "cfg", "seq", None),
            P("req", "cfg", "seq", None),
            P("req", "cfg", "seq", None),
            P("req", None),
            P(),
            P(),
            P("req", None),
            P("req", None, None),
            P("req", None),
            P("req"),
            P("req"),
            P("req", "seq", "cfg"),
        ),
        out_specs=(P("req", "seq", "cfg"), P("req", "seq", "cfg")),
        check_vma=False,
    )
```
